32 devices in a mesh: toa: 16 (over z, y, x), rep: 2 (over core).
Axes of the slice: x: 2, y: 2, z: 4, core: 2. Of those that a mesh axis runs over, the one named last changes fastest.
Arguments:
- residual: float32 [2048, 256], P('toa'), may hold values from -6 to 6
- toa_error: float32 [2048, 256], P('toa'), may hold values from 0.3 to 3
- basis_rows: bfloat16 [2048, 100, 256], P('toa', 'rep'), may hold values from -0.041432038 to 0.041432038
- efac_table: float32 [16, 64], replicated, may hold values from 0.5 to 2
- equad_table: float32 [16, 64], replicated, may hold values from 0.1 to 1
- pulsar: int32 [2048], P('toa'), may hold values from 0 to 15
- backend: int32 [2048], P('toa'), may hold values from 0 to 63
- counts: int32 [2048], P('toa'), may hold values from 64 to 256
- owner_slot: int32 [2048], P('toa'), may hold values from 0 to 2047, as said below
Outputs:
- gram_matrix: float32 [16, 100, 100], P('toa', None, 'rep')
- projection: float32 [16, 100], P('toa', 'rep')
- whitened: float32 [2048, 256], P('toa')
The draws below stay inside these ranges and needn't reach their ends.
Inputs may be any that keep to these rules, and one draw needn't show every extreme that they name: A permutation of the 2048 slots, independent of pulsar and backend; owner_slot // 128 is the device index along toa that holds the tile's output row and owner_slot % 128 its place there; each device's tiles go exactly 8 to each device.
All inputs are finite; a program needn't handle non-finite values.
Results may differ from the reference program's by a relative error of at most 0.0032.
Values may be sent and summed in bfloat16 or wider, within the bound.
A program may use at most 64 MiB of HBM per device.

```python
import math
import jax
import jax.numpy as jnp
import numpy as np
from jax import lax

K = 100
B = 64
ROWS = 256
TILES_DEV = 128
PSR_DEV = 1
P_SIZE = 16
TILES = 2048


def draw_basis_rows(key, part):
    noise_key, column_key = jax.random.split(jax.random.fold_in(key, 11))
    spread = 1.0 / math.sqrt(TILES_DEV * ROWS // PSR_DEV)
    noise = jnp.clip(jax.random.normal(noise_key, (TILES, K, ROWS), jnp.float32), -6.0, 6.0)
    column_mean = jax.random.uniform(column_key, (K,), jnp.float32, -1.0, 1.0)
    values = (noise + column_mean[None, :, None]) * spread
    return values.astype(jnp.bfloat16)


def draw_owner_slot(key, part):
    source_key, dest_key = jax.random.split(jax.random.fold_in(key, 23))
    peer_count = TILES // TILES_DEV
    per_peer = TILES_DEV // peer_count
    source_order = jax.vmap(lambda small_key: jax.random.permutation(small_key, TILES_DEV))(jax.random.split(source_key, peer_count))
    dest_order = jax.vmap(lambda small_key: jax.random.permutation(small_key, TILES_DEV))(jax.random.split(dest_key, peer_count))
    source_ids = jnp.arange(peer_count, dtype=jnp.int32)[:, None, None]
    dest_ids = jnp.arange(peer_count, dtype=jnp.int32)[None, :, None]
    copy_ids = jnp.arange(per_peer, dtype=jnp.int32)[None, None, :]
    tile_index = source_ids * TILES_DEV + source_order[source_ids, dest_ids * per_peer + copy_ids]
    slot_value = dest_ids * TILES_DEV + dest_order[dest_ids, source_ids * per_peer + copy_ids]
    tile_index = jnp.broadcast_to(tile_index, (peer_count, peer_count, per_peer)).reshape(-1)
    slot_value = jnp.broadcast_to(slot_value, (peer_count, peer_count, per_peer)).reshape(-1)
    return jnp.zeros((TILES,), jnp.int32).at[tile_index].set(slot_value.astype(jnp.int32))


def touch_ends(array, stream_key, low, top_value):
    spot = [jax.random.randint(jax.random.fold_in(stream_key, axis), (), 0, length) for axis, length in enumerate(array.shape)]
    longest = array.shape.index(max(array.shape))
    next_to = spot[:longest] + [(spot[longest] + 1) % array.shape[longest]] + spot[longest + 1:]
    return array.at[tuple(spot)].set(low).at[tuple(next_to)].set(top_value)


def level_of(key, shape, cuts, smallest, top_value):
    factor_of = 1.0
    for position, blocks in cuts:
        heights = jax.random.uniform(jax.random.fold_in(jax.random.fold_in(key, 6), position), (blocks,), jnp.float32, smallest / len(cuts), top_value / len(cuts))
        factor_of = factor_of * jnp.repeat(jnp.exp(heights), shape[position] // blocks).reshape((-1,) + (1,) * (len(shape) - 1 - position))
    return factor_of


def cumulative_ranks(amount, slope):
    portions = [(1 << 20) // math.isqrt(standing ** slope) + 1 for standing in range(1, amount + 1)]
    width = 1 + sum(portions) // (1 << 30)
    return np.cumsum(np.array([max(1, weight // width) for weight in portions]))


def ranked(stream_key, extent, amount, skew):
    grid = cumulative_ranks(amount, skew)
    pick = jax.random.randint(jax.random.fold_in(stream_key, 1), extent, 0, int(grid[amount - 1]))
    grade = jnp.searchsorted(jnp.asarray(grid, jnp.int32), pick, side="right")
    return jax.random.permutation(jax.random.fold_in(stream_key, 2), amount)[grade].astype(jnp.int32)


def scatter_about(own_key, shape, width, most, cuts=(), kind=jnp.bfloat16):
    loudness = level_of(own_key, shape, cuts, -0.22, 0.18) if cuts else 1.0
    result = jax.random.normal(own_key, shape, jnp.float32) * width * loudness
    return jnp.minimum(jnp.maximum(result, -most), most).astype(kind)


def setup_inputs(seed: int = 0) -> dict:
    splits = jax.random.split(jax.random.key(seed), 10)
    residual = scatter_about(splits[0], (TILES, ROWS), 1.0, 6.0, ((0, 16),), jnp.float32)
    toa_error = jnp.clip(jnp.exp(math.log(3.0) - 2.3025851 * jax.random.uniform(splits[1], (TILES, ROWS), jnp.float32) ** level_of(splits[1], (TILES, ROWS), ((0, 16),), -0.2, 0.2)), 0.3, 3.0)
    basis_rows = draw_basis_rows(jax.random.fold_in(splits[9], 71), 0)
    efac_table = jnp.clip(jnp.exp(jax.random.uniform(splits[3], (P_SIZE, B), jnp.float32, math.log(0.5), math.log(2.0))), 0.5, 2.0)
    equad_table = jnp.clip(jnp.exp(jax.random.uniform(splits[4], (P_SIZE, B), jnp.float32, math.log(0.1), math.log(1.0))), 0.1, 1.0)
    pulsar = touch_ends(ranked(splits[5], (TILES,), P_SIZE, 1), jax.random.fold_in(splits[5], 3), 0, P_SIZE - 1).astype(jnp.int32)
    backend = touch_ends(jax.random.randint(splits[6], (TILES,), 0, B), jax.random.fold_in(splits[6], 1), 0, B - 1).astype(jnp.int32)
    counts = touch_ends(jax.random.randint(splits[7], (TILES,), ROWS // 4, ROWS + 1), jax.random.fold_in(splits[7], 1), ROWS // 4, ROWS).astype(jnp.int32)
    owner_slot = draw_owner_slot(jax.random.fold_in(splits[9], 71), 0)
    return {"residual": residual, "toa_error": toa_error, "basis_rows": basis_rows, "efac_table": efac_table, "equad_table": equad_table, "pulsar": pulsar, "backend": backend, "counts": counts, "owner_slot": owner_slot}


def reference(residual, toa_error, basis_rows, efac_table, equad_table, pulsar, backend, counts, owner_slot):
    factor = efac_table[pulsar, backend]
    floor_term = equad_table[pulsar, backend]
    valid_rows = jnp.arange(ROWS, dtype=jnp.int32)[None, :] < counts[:, None]
    weight = jnp.where(valid_rows, 1.0 / (factor[:, None] ** 2 * toa_error ** 2 + floor_term[:, None] ** 2), 0.0).astype(jnp.float32)
    whitened_local = jnp.sqrt(weight) * residual
    whitened = jnp.zeros_like(whitened_local).at[owner_slot.astype(jnp.int32)].set(whitened_local)
    block_count = TILES // TILES_DEV
    basis_blocks = basis_rows.reshape(block_count, TILES_DEV, K, ROWS)
    weight_blocks = weight.reshape(block_count, TILES_DEV, ROWS)
    residual_blocks = residual.reshape(block_count, TILES_DEV, ROWS)
    pulsar_blocks = pulsar.reshape(block_count, TILES_DEV)
    high = lax.Precision.HIGHEST

    def step_fn(carry, inputs):
        gram_sum, proj_sum = carry
        basis_block, weight_block, residual_block, pulsar_block = inputs
        basis_float = basis_block.astype(jnp.float32)
        scaled = lax.optimization_barrier((weight_block[:, None, :] * basis_float).astype(jnp.bfloat16)).astype(jnp.float32)
        weighted_res = lax.optimization_barrier((weight_block * residual_block).astype(jnp.bfloat16)).astype(jnp.float32)
        tile_gram = jnp.einsum('tkr,tjr->tkj', basis_float, scaled, precision=high)
        tile_proj = jnp.einsum('tkr,tr->tk', basis_float, weighted_res, precision=high)
        onehot = (pulsar_block[:, None] == jnp.arange(P_SIZE, dtype=jnp.int32)[None, :]).astype(jnp.float32)
        gram_sum = gram_sum + jnp.einsum('tp,tkj->pkj', onehot, tile_gram, precision=high)
        proj_sum = proj_sum + jnp.einsum('tp,tk->pk', onehot, tile_proj, precision=high)
        return ((gram_sum, proj_sum), None)
    initial = (jnp.zeros((P_SIZE, K, K), jnp.float32), jnp.zeros((P_SIZE, K), jnp.float32))
    (gram_matrix, projection), unused = lax.scan(step_fn, initial, (basis_blocks, weight_blocks, residual_blocks, pulsar_blocks))
    return (gram_matrix, projection, whitened)
```

```python
import functools

import jax
import jax.numpy as jnp
from jax import lax
from jax.experimental import pallas as pl
from jax.experimental.pallas import tpu as pltpu
from jax.sharding import PartitionSpec as P

MESH = pl.DeviceIdType.MESH
GROUP = 16
LANES = 128


def round_up(value, step):
    return (value + step - 1) // step * step


def local_kernel(
    peers,
    pulsar_ref,
    backend_ref,
    counts_ref,
    slot_ref,
    efac_ref,
    equad_ref,
    residual_ref,
    error_ref,
    own_ref,
    other_ref,
    rows_ref,
    part_ref,
    total,
    filled,
):
    step = pl.program_id(0)
    half, group, row_total = own_ref.shape
    pulsar_total = total.shape[0]
    tile_total = group * pl.num_programs(0)
    per_peer = tile_total // peers

    @pl.when(step == 0)
    def _():
        total[...] = jnp.zeros_like(total)

        def clear(i, carry):
            filled[i] = 0
            return carry

        lax.fori_loop(0, peers, clear, 0)

    def tiles_first(ref):
        block = ref[...].astype(jnp.float32)
        block = jnp.concatenate(
            [block, jnp.zeros((round_up(half + 2, 8) - half, group, row_total), jnp.float32)], axis=0
        )
        return jnp.swapaxes(block, 0, 1)

    own = tiles_first(own_ref)
    other = tiles_first(other_ref)
    lane = lax.broadcasted_iota(jnp.int32, (1, row_total), 1)
    below = lax.broadcasted_iota(jnp.int32, (own.shape[1], row_total), 0)
    for i in range(group):
        tile = step * group + i
        p = pulsar_ref[tile]
        b = backend_ref[tile]
        factor = efac_ref[p, b]
        floor_term = equad_ref[p, b]
        residual = residual_ref[i : i + 1, :]
        error = error_ref[i : i + 1, :]
        weight = jnp.where(
            lane < counts_ref[tile],
            1.0 / (factor * factor * (error * error) + floor_term * floor_term),
            0.0,
        )
        slot = slot_ref[tile]
        dest = slot // tile_total
        rank = filled[dest]
        filled[dest] = rank + 1
        place = (slot - dest * tile_total).astype(jnp.float32)
        position = dest * per_peer + rank
        white = jnp.sqrt(weight) * residual
        for c in range(row_total // LANES):
            rows_ref[position, c : c + 1, :] = white[:, c * LANES : (c + 1) * LANES]
        rows_ref[position, row_total // LANES :, :] = jnp.full((1, LANES), place, jnp.float32)
        basis = own[i]
        left = jnp.where(below == half, weight * residual, weight * basis).astype(jnp.bfloat16)
        right = jnp.concatenate([basis, other[i]], axis=0).astype(jnp.bfloat16)
        gram = lax.dot_general(
            left, right, (((1,), (1,)), ((), ())), preferred_element_type=jnp.float32
        )
        total[p] += gram

    @pl.when(step == pl.num_programs(0) - 1)
    def _():
        def narrow(q, carry):
            block = total[q]
            high = block.astype(jnp.bfloat16)
            rest = block - high.astype(jnp.float32)
            index = lax.broadcasted_iota(jnp.int32, block.shape, 0)
            shifted = pltpu.roll(rest, 1, 0)
            part_ref[q] = jnp.where(index == half + 1, shifted, high.astype(jnp.float32)).astype(
                jnp.bfloat16
            )
            return carry

        lax.fori_loop(0, pulsar_total, narrow, 0)


def exchange_kernel(
    peers,
    half,
    rows_ref,
    part_ref,
    white_ref,
    gram_ref,
    got_rows,
    got_part,
    sends,
    arrivals,
):
    me = lax.axis_index("toa")
    owned = part_ref.shape[0] // peers
    tile_total = white_ref.shape[0]
    row_total = white_ref.shape[1]
    barrier = pltpu.get_barrier_semaphore()
    for d in range(1, peers):
        pl.semaphore_signal(
            barrier, inc=1, device_id={"toa": lax.rem(me + d, peers)}, device_id_type=MESH
        )
    pl.semaphore_wait(barrier, peers - 1)

    def copies(d):
        peer = lax.rem(me + d, peers)
        first = pltpu.make_async_remote_copy(
            src_ref=part_ref.at[pl.ds(peer * owned, owned)],
            dst_ref=got_part.at[d],
            send_sem=sends.at[0, d],
            recv_sem=arrivals.at[0, d],
            device_id={"toa": peer},
            device_id_type=MESH,
        )
        second = pltpu.make_async_remote_copy(
            src_ref=rows_ref.at[peer],
            dst_ref=got_rows.at[d],
            send_sem=sends.at[1, d],
            recv_sem=arrivals.at[1, d],
            device_id={"toa": peer},
            device_id_type=MESH,
        )
        return (first, second)

    def start(d, carry):
        for copy in copies(d):
            copy.start()
        return carry

    def finish(d, carry):
        for copy in copies(d):
            copy.wait()
        return carry

    lax.fori_loop(1, peers, start, 0)
    got_rows[0] = rows_ref[me]
    got_part[0] = part_ref[pl.ds(me * owned, owned)]
    lax.fori_loop(1, peers, finish, 0)

    summed = lax.fori_loop(
        0,
        peers,
        lambda d, acc: acc + got_part[d].astype(jnp.float32),
        jnp.zeros(got_part.shape[1:], jnp.float32),
    )
    gram_ref[...] = summed
    chunks = row_total // LANES
    places = got_rows[:, :, chunks, :].reshape(tile_total, LANES)
    data = jnp.concatenate(
        [got_rows[:, :, c, :].reshape(tile_total, LANES) for c in range(chunks)], axis=1
    )
    for first in range(0, tile_total, LANES):
        spot = first + lax.broadcasted_iota(jnp.int32, (tile_total, LANES), 1)
        chosen = (places == spot.astype(jnp.float32)).astype(jnp.float32)
        white_ref[first : first + LANES, :] = lax.dot_general(
            chosen,
            data,
            (((0,), (0,)), ((), ())),
            precision=lax.Precision.HIGHEST,
            preferred_element_type=jnp.float32,
        )


def shards(
    residual, toa_error, basis_rows, efac_table, equad_table, pulsar, backend, counts, owner_slot
):
    tile_total, row_total = residual.shape
    peers = lax.axis_size("toa")
    half = basis_rows.shape[1]
    pulsar_total = efac_table.shape[0]
    owned = pulsar_total // peers
    per_peer = tile_total // peers
    padded = round_up(half + 2, 8)
    pieces = row_total // LANES + 1
    group = min(GROUP, tile_total)
    own = jnp.transpose(basis_rows, (1, 0, 2))
    other = lax.ppermute(own, "rep", [(0, 1), (1, 0)])
    smem = pl.BlockSpec(memory_space=pltpu.SMEM)
    rows, parts = pl.pallas_call(
        functools.partial(local_kernel, peers),
        grid=(tile_total // group,),
        in_specs=[smem] * 6
        + [pl.BlockSpec((group, row_total), lambda i: (i, 0))] * 2
        + [pl.BlockSpec((half, group, row_total), lambda i: (0, i, 0))] * 2,
        out_specs=[
            pl.BlockSpec((tile_total, pieces, LANES), lambda i: (0, 0, 0)),
            pl.BlockSpec((pulsar_total, padded, 2 * padded), lambda i: (0, 0, 0)),
        ],
        out_shape=[
            jax.ShapeDtypeStruct((tile_total, pieces, LANES), jnp.float32),
            jax.ShapeDtypeStruct((pulsar_total, padded, 2 * padded), jnp.bfloat16),
        ],
        scratch_shapes=[
            pltpu.VMEM((pulsar_total, padded, 2 * padded), jnp.float32),
            pltpu.SMEM((peers,), jnp.int32),
        ],
        name="local_terms",
    )(
        pulsar,
        backend,
        counts,
        owner_slot,
        efac_table,
        equad_table,
        residual,
        toa_error,
        own,
        other,
    )
    vmem = pl.BlockSpec(memory_space=pltpu.VMEM)
    whitened, summed = pl.pallas_call(
        functools.partial(exchange_kernel, peers, half),
        in_specs=[vmem] * 2,
        out_specs=[vmem] * 2,
        out_shape=[
            jax.ShapeDtypeStruct((tile_total, row_total), jnp.float32),
            jax.ShapeDtypeStruct((owned, padded, 2 * padded), jnp.float32),
        ],
        scratch_shapes=[
            pltpu.VMEM((peers, per_peer, pieces, LANES), jnp.float32),
            pltpu.VMEM((peers, owned, padded, 2 * padded), jnp.bfloat16),
            pltpu.SemaphoreType.DMA((2, peers)),
            pltpu.SemaphoreType.DMA((2, peers)),
        ],
        compiler_params=pltpu.CompilerParams(collective_id=0, has_side_effects=True),
        name="exchange",
    )(rows.reshape(peers, per_peer, pieces, LANES), parts)
    projection = summed[:, half, :half] + summed[:, half + 1, :half]
    mine = summed[:, :half, :half]
    theirs = summed[:, :half, padded : padded + half]
    first_core = lax.axis_index("rep") == 0
    gram = jnp.concatenate(
        [jnp.where(first_core, mine, theirs), jnp.where(first_core, theirs, mine)], axis=2
    )
    return (jnp.transpose(gram, (0, 2, 1)), projection, whitened)


def solution(mesh):
    in_specs = (
        P("toa", None),
        P("toa", None),
        P("toa", "rep", None),
        P(),
        P(),
        P("toa"),
        P("toa"),
        P("toa"),
        P("toa"),
    )
    out_specs = (P("toa", None, "rep"), P("toa", "rep"), P("toa", None))
    return jax.shard_map(shards, mesh=mesh, in_specs=in_specs, out_specs=out_specs, check_vma=False)
```

```python
import functools

import jax
import jax.numpy as jnp
from jax import lax
from jax.experimental import pallas as pl
from jax.experimental.pallas import tpu as pltpu
from jax.sharding import PartitionSpec as P

MESH = pl.DeviceIdType.MESH
GROUP = 16
LANES = 128
VMEM_ALL = 67043328
HIGH = lax.Precision.HIGHEST


def round_up(value, step):
    return (value + step - 1) // step * step


def meet(peers, me):
    barrier = pltpu.get_barrier_semaphore()

    def greet(d, carry):
        pl.semaphore_signal(
            barrier, inc=1, device_id={"toa": lax.rem(me + d, peers)}, device_id_type=MESH
        )
        return carry

    lax.fori_loop(1, peers, greet, 0)
    return barrier


def contract(left, right, dims, precision=None):
    return lax.dot_general(
        left, right, (dims, ((), ())), precision=precision, preferred_element_type=jnp.float32
    )


def spread_kernel(
    peers,
    pulsar_ref,
    backend_ref,
    counts_ref,
    slot_ref,
    efac_ref,
    equad_ref,
    residual_ref,
    error_ref,
    weight_ref,
    got_rows,
    got_places,
    sorted_rows,
    sorted_places,
    sends,
    arrivals,
    local_sem,
):
    me = lax.axis_index("toa")
    barrier = meet(peers, me)
    tile_total, row_total = residual_ref.shape
    per_peer = tile_total // peers

    def onehot(row, amount):
        index = lax.broadcasted_iota(jnp.int32, (amount, tile_total), 0)
        return (index == row).astype(jnp.float32)

    pulsar_hot = onehot(pulsar_ref[...], efac_ref.shape[0])
    backend_hot = onehot(backend_ref[...], efac_ref.shape[1])

    def lookup(ref):
        columns = contract(ref[...], pulsar_hot, ((0,), (0,)), HIGH)
        return jnp.sum(columns * backend_hot, axis=0, keepdims=True)

    factor = lookup(efac_ref)
    floor_term = lookup(equad_ref)
    slot = slot_ref[...]
    dest = slot // tile_total
    place = (slot - dest * tile_total).astype(jnp.float32)
    dest_hot = onehot(dest, peers)
    earlier = (
        lax.broadcasted_iota(jnp.int32, (tile_total, tile_total), 0)
        < lax.broadcasted_iota(jnp.int32, (tile_total, tile_total), 1)
    ).astype(jnp.float32)
    before = contract(dest_hot, earlier, ((1,), (0,)), HIGH)
    rank = jnp.sum(before * dest_hot, axis=0, keepdims=True)
    position = dest * per_peer + rank.astype(jnp.int32)
    order = onehot(position, tile_total)
    stacked = jnp.concatenate(
        [
            factor * factor,
            floor_term * floor_term,
            counts_ref[...].astype(jnp.float32),
            place,
            jnp.zeros((tile_total - 4, tile_total), jnp.float32),
        ],
        axis=0,
    )
    columns = jnp.transpose(stacked)
    lane = lax.broadcasted_iota(jnp.int32, (tile_total, row_total), 1).astype(jnp.float32)
    error = error_ref[...]
    weight = jnp.where(
        lane < columns[:, 2:3], 1.0 / (columns[:, 0:1] * (error * error) + columns[:, 1:2]), 0.0
    )
    weight_ref[...] = weight
    white = jnp.sqrt(weight) * residual_ref[...]
    sorted_rows[...] = contract(order, white, ((1,), (0,)), HIGH).reshape(sorted_rows.shape)
    sorted_places[...] = contract(place, order, ((1,), (1,)), HIGH).astype(jnp.int32)
    own_rows = pltpu.make_async_copy(sorted_rows.at[me], got_rows.at[0], local_sem.at[0])
    own_places = pltpu.make_async_copy(sorted_places, got_places.at[0], local_sem.at[1])
    own_rows.start()
    own_places.start()
    pl.semaphore_wait(barrier, peers - 1)

    def copies(d):
        peer = lax.rem(me + d, peers)
        pairs = ((sorted_rows.at[peer], got_rows.at[d]), (sorted_places, got_places.at[d]))
        return [
            pltpu.make_async_remote_copy(
                src_ref=source,
                dst_ref=target,
                send_sem=sends.at[n, d],
                recv_sem=arrivals.at[n, d],
                device_id={"toa": peer},
                device_id_type=MESH,
            )
            for n, (source, target) in enumerate(pairs)
        ]

    def start(d, carry):
        for copy in copies(d):
            copy.start()
        return carry

    def finish(d, carry):
        for copy in copies(d):
            copy.wait()
        return carry

    lax.fori_loop(1, peers, start, 0)
    own_rows.wait()
    own_places.wait()
    lax.fori_loop(1, peers, finish, 0)


def local_kernel(
    peers,
    pulsar_ref,
    places_ref,
    weight_ref,
    residual_ref,
    own_ref,
    other_ref,
    rows_ref,
    part_ref,
    white_ref,
    total,
    staged,
):
    step = pl.program_id(0)
    half, group, row_total = own_ref.shape
    pulsar_total, padded, width = total.shape
    me = lax.axis_index("toa")
    per_peer = rows_ref.shape[1]

    @pl.when(step == 0)
    def _():
        total[...] = jnp.zeros_like(total)

    def tiles_first(ref):
        block = ref[...].astype(jnp.float32)
        block = jnp.concatenate(
            [block, jnp.zeros((padded - half, group, row_total), jnp.float32)], axis=0
        )
        return jnp.swapaxes(block, 0, 1)

    own = tiles_first(own_ref)
    other = tiles_first(other_ref)
    below = lax.broadcasted_iota(jnp.int32, (padded, row_total), 0)
    for i in range(group):
        p = pulsar_ref[step * group + i]
        weight = weight_ref[i : i + 1, :]
        basis = own[i]
        left = jnp.where(below == half, residual_ref[i : i + 1, :], basis)
        left = (weight * left).astype(jnp.bfloat16)
        right = jnp.concatenate([basis, other[i]], axis=0).astype(jnp.bfloat16)
        total[p] += contract(left, right, ((1,), (1,)))

    source = step * (peers // pl.num_programs(0)) if peers % pl.num_programs(0) == 0 else None
    sources = range(peers // pl.num_programs(0)) if source is not None else ()

    def settle(d):
        for i in range(per_peer):
            place = places_ref[d, 0, me * per_peer + i]
            for c in range(row_total // LANES):
                staged[c, pl.ds(place, 1), :] = rows_ref[d, i : i + 1, c * LANES : (c + 1) * LANES]

    for s in sources:
        settle(source + s)

    @pl.when(step == pl.num_programs(0) - 1)
    def _():
        if source is None:

            def settle_one(d, carry):
                settle(d)
                return carry

            lax.fori_loop(0, peers, settle_one, 0)
        for c in range(row_total // LANES):
            white_ref[:, c * LANES : (c + 1) * LANES] = staged[c]

        def narrow(q, carry):
            block = total[q]
            high = block.astype(jnp.bfloat16).astype(jnp.float32)
            index = lax.broadcasted_iota(jnp.int32, block.shape, 0)
            shifted = pltpu.roll(block - high, 1, 0)
            part_ref[q] = jnp.where(index == half + 1, shifted, high).astype(jnp.bfloat16)
            return carry

        lax.fori_loop(0, pulsar_total, narrow, 0)


def gather_kernel(peers, part_ref, sum_ref, got_part, sends, arrivals):
    me = lax.axis_index("toa")
    owned = part_ref.shape[0] // peers
    barrier = meet(peers, me)
    pl.semaphore_wait(barrier, peers - 1)

    def copy_to(d):
        peer = lax.rem(me + d, peers)
        return pltpu.make_async_remote_copy(
            src_ref=part_ref.at[pl.ds(peer * owned, owned)],
            dst_ref=got_part.at[d],
            send_sem=sends.at[d],
            recv_sem=arrivals.at[d],
            device_id={"toa": peer},
            device_id_type=MESH,
        )

    def start(d, carry):
        copy_to(d).start()
        return carry

    def take(d, acc):
        copy_to(d).wait()
        return acc + got_part[d].astype(jnp.float32)

    lax.fori_loop(1, peers, start, 0)
    mine = part_ref[pl.ds(me * owned, owned)].astype(jnp.float32)
    sum_ref[...] = lax.fori_loop(1, peers, take, mine)


def finish_kernel(half, sum_ref, gram_ref, projection_ref):
    first_core = lax.axis_index("rep") == 0
    padded = sum_ref.shape[1]
    for q in range(sum_ref.shape[0]):
        block = sum_ref[q]
        projection_ref[q : q + 1, :] = (
            block[half : half + 1, :half] + block[half + 1 : half + 2, :half]
        )
        mine = block[:half, :half]
        theirs = block[:half, padded : padded + half]
        gram_ref[:, q, :half] = jnp.where(first_core, mine, theirs)
        gram_ref[:, q, half:] = jnp.where(first_core, theirs, mine)


def shards(
    residual, toa_error, basis_rows, efac_table, equad_table, pulsar, backend, counts, owner_slot
):
    tile_total, row_total = residual.shape
    peers = lax.axis_size("toa")
    half = basis_rows.shape[1]
    pulsar_total = efac_table.shape[0]
    owned = pulsar_total // peers
    per_peer = tile_total // peers
    padded = round_up(half + 2, 8)
    width = 2 * padded
    group = min(GROUP, tile_total)
    steps = tile_total // group
    chunks = row_total // LANES
    f32 = jnp.float32
    smem = pl.BlockSpec(memory_space=pltpu.SMEM)
    vmem = pl.BlockSpec(memory_space=pltpu.VMEM)
    own = jnp.transpose(basis_rows, (1, 0, 2))
    other = lax.ppermute(own, "rep", [(0, 1), (1, 0)])

    def row(vector):
        return vector.reshape(1, tile_total)

    weight, rows, places = pl.pallas_call(
        functools.partial(spread_kernel, peers),
        in_specs=[vmem] * 8,
        out_specs=[vmem] * 3,
        out_shape=[
            jax.ShapeDtypeStruct((tile_total, row_total), f32),
            jax.ShapeDtypeStruct((peers, per_peer, row_total), f32),
            jax.ShapeDtypeStruct((peers, 1, tile_total), jnp.int32),
        ],
        scratch_shapes=[
            pltpu.VMEM((peers, per_peer, row_total), f32),
            pltpu.VMEM((1, tile_total), jnp.int32),
            pltpu.SemaphoreType.DMA((2, peers)),
            pltpu.SemaphoreType.DMA((2, peers)),
            pltpu.SemaphoreType.DMA((2,)),
        ],
        compiler_params=pltpu.CompilerParams(collective_id=1, has_side_effects=True),
        cost_estimate=pl.CostEstimate(
            flops=16 * tile_total * tile_total * row_total,
            bytes_accessed=5 * 4 * tile_total * row_total,
            transcendentals=tile_total * row_total,
        ),
        name="spread",
    )(
        row(pulsar),
        row(backend),
        row(counts),
        row(owner_slot),
        efac_table,
        equad_table,
        residual,
        toa_error,
    )
    parts, whitened = pl.pallas_call(
        functools.partial(local_kernel, peers),
        grid=(steps,),
        in_specs=[smem] * 2
        + [pl.BlockSpec((group, row_total), lambda i: (i, 0))] * 2
        + [pl.BlockSpec((half, group, row_total), lambda i: (0, i, 0))] * 2
        + [pl.BlockSpec((peers, per_peer, row_total), lambda i: (0, 0, 0))],
        out_specs=[
            pl.BlockSpec((pulsar_total, padded, width), lambda i: (0, 0, 0)),
            pl.BlockSpec((tile_total, row_total), lambda i: (0, 0)),
        ],
        out_shape=[
            jax.ShapeDtypeStruct((pulsar_total, padded, width), jnp.bfloat16),
            jax.ShapeDtypeStruct((tile_total, row_total), f32),
        ],
        scratch_shapes=[
            pltpu.VMEM((pulsar_total, padded, width), f32),
            pltpu.VMEM((chunks, tile_total, LANES), f32),
        ],
        compiler_params=pltpu.CompilerParams(vmem_limit_bytes=VMEM_ALL),
        name="local_terms",
    )(pulsar, places, weight, residual, own, other, rows)
    summed = pl.pallas_call(
        functools.partial(gather_kernel, peers),
        in_specs=[vmem],
        out_specs=vmem,
        out_shape=jax.ShapeDtypeStruct((owned, padded, width), f32),
        scratch_shapes=[
            pltpu.VMEM((peers, owned, padded, width), jnp.bfloat16),
            pltpu.SemaphoreType.DMA((peers,)),
            pltpu.SemaphoreType.DMA((peers,)),
        ],
        compiler_params=pltpu.CompilerParams(collective_id=0, has_side_effects=True),
        name="gather_parts",
    )(parts)
    gram, projection = pl.pallas_call(
        functools.partial(finish_kernel, half),
        in_specs=[vmem],
        out_specs=[vmem] * 2,
        out_shape=[
            jax.ShapeDtypeStruct((half, owned, 2 * half), f32),
            jax.ShapeDtypeStruct((owned, half), f32),
        ],
        name="finish",
    )(summed)
    return (jnp.transpose(gram, (1, 2, 0)), projection, whitened)


def solution(mesh):
    in_specs = (
        P("toa", None),
        P("toa", None),
        P("toa", "rep", None),
        P(),
        P(),
        P("toa"),
        P("toa"),
        P("toa"),
        P("toa"),
    )
    out_specs = (P("toa", None, "rep"), P("toa", "rep"), P("toa", None))
    return jax.shard_map(shards, mesh=mesh, in_specs=in_specs, out_specs=out_specs, check_vma=False)
```

```python
import functools

import jax
import jax.numpy as jnp
from jax import lax
from jax.experimental import pallas as pl
from jax.experimental.pallas import tpu as pltpu
from jax.sharding import PartitionSpec as P

MESH = pl.DeviceIdType.MESH
GROUP = 16
LANES = 128
VMEM_ALL = 67043328
HIGH = lax.Precision.HIGHEST


def round_up(value, step):
    return (value + step - 1) // step * step


def contract(left, right, dims, precision=None):
    return lax.dot_general(
        left, right, (dims, ((), ())), precision=precision, preferred_element_type=jnp.float32
    )


def whole_kernel(
    peers,
    pulsar_ref,
    backend_ref,
    counts_ref,
    slot_ref,
    efac_ref,
    equad_ref,
    residual_ref,
    error_ref,
    basis_ref,
    sum_ref,
    got_rows,
    got_places,
    sorted_rows,
    sorted_places,
    own_store,
    other_store,
    weights,
    lefts,
    owns,
    grams,
    part_wide,
    part,
    got_part,
    load_sems,
    swap_sends,
    swap_arrivals,
    sends,
    arrivals,
    local_sem,
):
    me = lax.axis_index("toa")
    partner = 1 - lax.axis_index("rep")
    half, tile_total, row_total = basis_ref.shape
    padded = lefts.shape[1]
    pulsar_total = efac_ref.shape[0]
    owned = pulsar_total // peers
    per_peer = tile_total // peers
    group = min(GROUP, tile_total)
    steps = tile_total // group

    barrier = pltpu.get_barrier_semaphore()
    pl.semaphore_signal(barrier, inc=1, device_id={"rep": partner}, device_id_type=MESH)

    def greet(d, carry):
        pl.semaphore_signal(
            barrier, inc=1, device_id={"toa": lax.rem(me + d, peers)}, device_id_type=MESH
        )
        return carry

    lax.fori_loop(1, peers, greet, 0)

    def chunk(ref, g):
        return ref.at[:, pl.ds(pl.multiple_of(g * group, group), group), :]

    def load(g):
        return pltpu.make_async_copy(chunk(basis_ref, g), chunk(own_store, g), load_sems.at[g])

    def swap(g):
        return pltpu.make_async_remote_copy(
            src_ref=chunk(basis_ref, g),
            dst_ref=chunk(other_store, g),
            send_sem=swap_sends.at[g],
            recv_sem=swap_arrivals.at[g],
            device_id={"rep": partner},
            device_id_type=MESH,
        )

    def each(first, last, action):
        def body(i, carry):
            action(i)
            return carry

        lax.fori_loop(first, last, body, 0)

    each(0, steps, lambda g: load(g).start())

    def onehot(row, amount):
        index = lax.broadcasted_iota(jnp.int32, (amount, tile_total), 0)
        return (index == row).astype(jnp.float32)

    pulsar_hot = onehot(pulsar_ref[...], pulsar_total)
    backend_hot = onehot(backend_ref[...], efac_ref.shape[1])

    def lookup(ref):
        columns = contract(ref[...], pulsar_hot, ((0,), (0,)), HIGH)
        return jnp.sum(columns * backend_hot, axis=0, keepdims=True)

    factor = lookup(efac_ref)
    floor_term = lookup(equad_ref)
    slot = slot_ref[...]
    dest = slot // tile_total
    place = (slot - dest * tile_total).astype(jnp.float32)
    dest_hot = onehot(dest, peers)
    earlier = (
        lax.broadcasted_iota(jnp.int32, (tile_total, tile_total), 0)
        < lax.broadcasted_iota(jnp.int32, (tile_total, tile_total), 1)
    ).astype(jnp.float32)
    before = contract(dest_hot, earlier, ((1,), (0,)))
    rank = jnp.sum(before * dest_hot, axis=0, keepdims=True)
    position = dest * per_peer + rank.astype(jnp.int32)
    order = onehot(position, tile_total)
    stacked = jnp.concatenate(
        [
            factor * factor,
            floor_term * floor_term,
            counts_ref[...].astype(jnp.float32),
            jnp.zeros((tile_total - 3, tile_total), jnp.float32),
        ],
        axis=0,
    )
    columns = jnp.transpose(stacked)
    lane = lax.broadcasted_iota(jnp.int32, (tile_total, row_total), 1).astype(jnp.float32)
    error = error_ref[...]
    weight = jnp.where(
        lane < columns[:, 2:3], 1.0 / (columns[:, 0:1] * (error * error) + columns[:, 1:2]), 0.0
    )
    weights[...] = weight
    white = jnp.sqrt(weight) * residual_ref[...]
    sorted_rows[...] = contract(order, white, ((1,), (0,)), HIGH).reshape(sorted_rows.shape)
    sorted_places[...] = contract(place, order, ((1,), (1,)), HIGH).astype(jnp.int32)
    own_rows = pltpu.make_async_copy(sorted_rows.at[me], got_rows.at[0], local_sem.at[0])
    own_places = pltpu.make_async_copy(sorted_places, got_places.at[0], local_sem.at[1])
    own_rows.start()
    own_places.start()
    pl.semaphore_wait(barrier, peers)

    def remote(source, target, n, d):
        return pltpu.make_async_remote_copy(
            src_ref=source,
            dst_ref=target,
            send_sem=sends.at[n, d],
            recv_sem=arrivals.at[n, d],
            device_id={"toa": lax.rem(me + d, peers)},
            device_id_type=MESH,
        )

    def rows_to(d):
        return remote(sorted_rows.at[lax.rem(me + d, peers)], got_rows.at[d], 0, d)

    def places_to(d):
        return remote(sorted_places, got_places.at[d], 1, d)

    def part_to(d):
        first = lax.rem(me + d, peers) * owned
        return remote(part.at[pl.ds(first, owned)], got_part.at[d], 2, d)

    each(0, steps, lambda g: swap(g).start())

    def send_rows(d):
        rows_to(d).start()
        places_to(d).start()

    each(1, peers, send_rows)

    def tiles_first(ref, g):
        block = chunk(ref, g)[...].astype(jnp.float32)
        block = jnp.concatenate(
            [block, jnp.zeros((padded - half, group, row_total), jnp.float32)], axis=0
        )
        return jnp.swapaxes(block, 0, 1)

    below = lax.broadcasted_iota(jnp.int32, (padded, row_total), 0)

    def prepare(g):
        load(g).wait()
        own = tiles_first(own_store, g)
        start = pl.multiple_of(g * group, group)
        weight = weights[pl.ds(start, group), :]
        residual = residual_ref[pl.ds(start, group), :]
        for i in range(group):
            basis = own[i]
            left = weight[i : i + 1, :] * jnp.where(below == half, residual[i : i + 1, :], basis)
            lefts[start + i] = left.astype(jnp.bfloat16)
            owns[start + i] = basis.astype(jnp.bfloat16)

    each(0, steps, prepare)

    def multiply(g):
        swap(g).wait()
        other = tiles_first(other_store, g).astype(jnp.bfloat16)
        start = pl.multiple_of(g * group, group)
        for i in range(group):
            right = jnp.concatenate([owns[start + i], other[i]], axis=0)
            grams[start + i] = contract(lefts[start + i], right, ((1,), (1,)))

    each(0, steps, multiply)

    chosen = pulsar_hot.astype(jnp.bfloat16)
    for j in range(half + 1):
        terms = grams[:, j, :]
        high = terms.astype(jnp.bfloat16)
        low = (terms - high.astype(jnp.float32)).astype(jnp.bfloat16)
        summed = contract(chosen, high, ((1,), (0,))) + contract(chosen, low, ((1,), (0,)))
        if j == half:
            coarse = summed.astype(jnp.bfloat16).astype(jnp.float32)
            part_wide[:, j, :] = coarse
            part_wide[:, j + 1, :] = summed - coarse
        else:
            part_wide[:, j, :] = summed
    for j in range(half + 2, padded):
        part_wide[:, j, :] = jnp.zeros((pulsar_total, part_wide.shape[2]), jnp.float32)
    part[...] = part_wide[...].astype(jnp.bfloat16)
    each(1, peers, lambda d: part_to(d).start())
    own_rows.wait()
    own_places.wait()

    def take_rows(d):
        rows_to(d).wait()
        places_to(d).wait()

    each(1, peers, take_rows)

    def take(d, acc):
        part_to(d).wait()
        return acc + got_part[d].astype(jnp.float32)

    mine = part[pl.ds(me * owned, owned)].astype(jnp.float32)
    sum_ref[...] = lax.fori_loop(1, peers, take, mine)


def finish_kernel(
    peers,
    half,
    places_ref,
    sum_ref,
    rows_ref,
    gram_ref,
    projection_ref,
    white_ref,
    staged,
):
    first_core = lax.axis_index("rep") == 0
    me = lax.axis_index("toa")
    padded = sum_ref.shape[1]
    per_peer, row_total = rows_ref.shape[1:]
    chunks = row_total // LANES

    def settle(d, carry):
        for i in range(per_peer):
            place = places_ref[d, 0, me * per_peer + i]
            for c in range(chunks):
                staged[c, pl.ds(place, 1), :] = rows_ref[d, i : i + 1, c * LANES : (c + 1) * LANES]
        return carry

    lax.fori_loop(0, peers, settle, 0)
    for c in range(chunks):
        white_ref[:, c * LANES : (c + 1) * LANES] = staged[c]
    for q in range(sum_ref.shape[0]):
        block = sum_ref[q]
        projection_ref[q : q + 1, :] = (
            block[half : half + 1, :half] + block[half + 1 : half + 2, :half]
        )
        mine = block[:half, :half]
        theirs = block[:half, padded : padded + half]
        gram_ref[:, q, :half] = jnp.where(first_core, mine, theirs)
        gram_ref[:, q, half:] = jnp.where(first_core, theirs, mine)


def shards(
    residual, toa_error, basis_rows, efac_table, equad_table, pulsar, backend, counts, owner_slot
):
    tile_total, row_total = residual.shape
    peers = lax.axis_size("toa")
    half = basis_rows.shape[1]
    pulsar_total = efac_table.shape[0]
    owned = pulsar_total // peers
    per_peer = tile_total // peers
    padded = round_up(half + 2, 8)
    width = 2 * padded
    steps = tile_total // min(GROUP, tile_total)
    f32 = jnp.float32
    bf16 = jnp.bfloat16
    smem = pl.BlockSpec(memory_space=pltpu.SMEM)
    vmem = pl.BlockSpec(memory_space=pltpu.VMEM)

    def row(vector):
        return vector.reshape(1, tile_total)

    summed, rows, places = pl.pallas_call(
        functools.partial(whole_kernel, peers),
        in_specs=[vmem] * 8 + [pl.BlockSpec(memory_space=pl.ANY)],
        out_specs=[vmem] * 3,
        out_shape=[
            jax.ShapeDtypeStruct((owned, padded, width), f32),
            jax.ShapeDtypeStruct((peers, per_peer, row_total), f32),
            jax.ShapeDtypeStruct((peers, 1, tile_total), jnp.int32),
        ],
        scratch_shapes=[
            pltpu.VMEM((peers, per_peer, row_total), f32),
            pltpu.VMEM((1, tile_total), jnp.int32),
            pltpu.VMEM((half, tile_total, row_total), bf16),
            pltpu.VMEM((half, tile_total, row_total), bf16),
            pltpu.VMEM((tile_total, row_total), f32),
            pltpu.VMEM((tile_total, padded, row_total), bf16),
            pltpu.VMEM((tile_total, padded, row_total), bf16),
            pltpu.VMEM((tile_total, padded, width), f32),
            pltpu.VMEM((pulsar_total, padded, width), f32),
            pltpu.VMEM((pulsar_total, padded, width), bf16),
            pltpu.VMEM((peers, owned, padded, width), bf16),
            pltpu.SemaphoreType.DMA((steps,)),
            pltpu.SemaphoreType.DMA((steps,)),
            pltpu.SemaphoreType.DMA((steps,)),
            pltpu.SemaphoreType.DMA((3, peers)),
            pltpu.SemaphoreType.DMA((3, peers)),
            pltpu.SemaphoreType.DMA((2,)),
        ],
        compiler_params=pltpu.CompilerParams(
            collective_id=0, has_side_effects=True, vmem_limit_bytes=VMEM_ALL
        ),
        name="whole",
    )(
        row(pulsar),
        row(backend),
        row(counts),
        row(owner_slot),
        efac_table,
        equad_table,
        residual,
        toa_error,
        jnp.transpose(basis_rows, (1, 0, 2)),
    )
    gram, projection, whitened = pl.pallas_call(
        functools.partial(finish_kernel, peers, half),
        in_specs=[smem, vmem, vmem],
        out_specs=[vmem] * 3,
        out_shape=[
            jax.ShapeDtypeStruct((half, owned, 2 * half), f32),
            jax.ShapeDtypeStruct((owned, half), f32),
            jax.ShapeDtypeStruct((tile_total, row_total), f32),
        ],
        scratch_shapes=[pltpu.VMEM((row_total // LANES, tile_total, LANES), f32)],
        name="finish",
    )(places, summed, rows)
    return (jnp.transpose(gram, (1, 2, 0)), projection, whitened)


def solution(mesh):
    in_specs = (
        P("toa", None),
        P("toa", None),
        P("toa", "rep", None),
        P(),
        P(),
        P("toa"),
        P("toa"),
        P("toa"),
        P("toa"),
    )
    out_specs = (P("toa", None, "rep"), P("toa", "rep"), P("toa", None))
    return jax.shard_map(shards, mesh=mesh, in_specs=in_specs, out_specs=out_specs, check_vma=False)
```

```python
import functools

import jax
import jax.numpy as jnp
from jax import lax
from jax.experimental import pallas as pl
from jax.experimental.pallas import tpu as pltpu
from jax.sharding import PartitionSpec as P

MESH = pl.DeviceIdType.MESH
GROUP = 16
LANES = 128
VMEM_ALL = 67043328
HIGH = lax.Precision.HIGHEST


def round_up(value, step):
    return (value + step - 1) // step * step


def contract(left, right, dims, precision=None):
    return lax.dot_general(
        left, right, (dims, ((), ())), precision=precision, preferred_element_type=jnp.float32
    )


def whole_kernel(
    peers,
    pulsar_ref,
    backend_ref,
    counts_ref,
    slot_ref,
    efac_ref,
    equad_ref,
    residual_ref,
    error_ref,
    basis_ref,
    sum_ref,
    got_rows,
    got_places,
    sorted_rows,
    sorted_places,
    own_store,
    other_store,
    weights,
    lefts,
    owns,
    grams,
    part_wide,
    part,
    got_part,
    load_sems,
    swap_sends,
    swap_arrivals,
    sends,
    arrivals,
    local_sem,
):
    me = lax.axis_index("toa")
    partner = 1 - lax.axis_index("rep")
    half, tile_total, row_total = basis_ref.shape
    padded = lefts.shape[1]
    pulsar_total = efac_ref.shape[0]
    owned = pulsar_total // peers
    per_peer = tile_total // peers
    group = min(GROUP, tile_total)
    steps = tile_total // group

    barrier = pltpu.get_barrier_semaphore()
    pl.semaphore_signal(barrier, inc=1, device_id={"rep": partner}, device_id_type=MESH)

    def greet(d, carry):
        pl.semaphore_signal(
            barrier, inc=1, device_id={"toa": lax.rem(me + d, peers)}, device_id_type=MESH
        )
        return carry

    lax.fori_loop(1, peers, greet, 0)

    def chunk(ref, g):
        return ref.at[:, pl.ds(pl.multiple_of(g * group, group), group), :]

    def load(g):
        return pltpu.make_async_copy(chunk(basis_ref, g), chunk(own_store, g), load_sems.at[g])

    def swap(g):
        return pltpu.make_async_remote_copy(
            src_ref=chunk(basis_ref, g),
            dst_ref=chunk(other_store, g),
            send_sem=swap_sends.at[g],
            recv_sem=swap_arrivals.at[g],
            device_id={"rep": partner},
            device_id_type=MESH,
        )

    def each(first, last, action):
        def body(i, carry):
            action(i)
            return carry

        lax.fori_loop(first, last, body, 0)

    each(0, steps, lambda g: load(g).start())

    def onehot(row, amount):
        index = lax.broadcasted_iota(jnp.int32, (amount, tile_total), 0)
        return (index == row).astype(jnp.float32)

    pulsar_hot = onehot(pulsar_ref[...], pulsar_total)
    backend_hot = onehot(backend_ref[...], efac_ref.shape[1])

    def lookup(ref):
        columns = contract(ref[...], pulsar_hot, ((0,), (0,)), HIGH)
        return jnp.sum(columns * backend_hot, axis=0, keepdims=True)

    factor = lookup(efac_ref)
    floor_term = lookup(equad_ref)
    slot = slot_ref[...]
    dest = slot // tile_total
    place = (slot - dest * tile_total).astype(jnp.float32)
    dest_hot = onehot(dest, peers)
    earlier = (
        lax.broadcasted_iota(jnp.int32, (tile_total, tile_total), 0)
        < lax.broadcasted_iota(jnp.int32, (tile_total, tile_total), 1)
    ).astype(jnp.float32)
    before = contract(dest_hot, earlier, ((1,), (0,)))
    rank = jnp.sum(before * dest_hot, axis=0, keepdims=True)
    position = dest * per_peer + rank.astype(jnp.int32)
    order = onehot(position, tile_total)
    stacked = jnp.concatenate(
        [
            factor * factor,
            floor_term * floor_term,
            counts_ref[...].astype(jnp.float32),
            jnp.zeros((tile_total - 3, tile_total), jnp.float32),
        ],
        axis=0,
    )
    columns = jnp.transpose(stacked)
    lane = lax.broadcasted_iota(jnp.int32, (tile_total, row_total), 1).astype(jnp.float32)
    error = error_ref[...]
    weight = jnp.where(
        lane < columns[:, 2:3], 1.0 / (columns[:, 0:1] * (error * error) + columns[:, 1:2]), 0.0
    )
    weights[...] = weight
    white = jnp.sqrt(weight) * residual_ref[...]
    sorted_rows[...] = contract(order, white, ((1,), (0,)), HIGH).reshape(sorted_rows.shape)
    sorted_places[...] = contract(place, order, ((1,), (1,)), HIGH).astype(jnp.int32)
    own_rows = pltpu.make_async_copy(sorted_rows.at[me], got_rows.at[0], local_sem.at[0])
    own_places = pltpu.make_async_copy(sorted_places, got_places.at[0], local_sem.at[1])
    own_rows.start()
    own_places.start()
    pl.semaphore_wait(barrier, peers)

    def remote(source, target, n, d):
        return pltpu.make_async_remote_copy(
            src_ref=source,
            dst_ref=target,
            send_sem=sends.at[n, d],
            recv_sem=arrivals.at[n, d],
            device_id={"toa": lax.rem(me + d, peers)},
            device_id_type=MESH,
        )

    def rows_to(d):
        return remote(sorted_rows.at[lax.rem(me + d, peers)], got_rows.at[d], 0, d)

    def places_to(d):
        return remote(sorted_places, got_places.at[d], 1, d)

    def part_to(d):
        first = lax.rem(me + d, peers) * owned
        return remote(part.at[pl.ds(first, owned)], got_part.at[d], 2, d)

    each(0, steps, lambda g: swap(g).start())

    def send_rows(d):
        rows_to(d).start()
        places_to(d).start()

    each(1, peers, send_rows)

    def tiles_first(ref, g):
        block = chunk(ref, g)[...].astype(jnp.float32)
        block = jnp.concatenate(
            [block, jnp.zeros((padded - half, group, row_total), jnp.float32)], axis=0
        )
        return jnp.swapaxes(block, 0, 1)

    below = lax.broadcasted_iota(jnp.int32, (padded, row_total), 0)

    def prepare(g):
        load(g).wait()
        own = tiles_first(own_store, g)
        start = pl.multiple_of(g * group, group)
        weight = weights[pl.ds(start, group), :]
        residual = residual_ref[pl.ds(start, group), :]
        for i in range(group):
            basis = own[i]
            left = weight[i : i + 1, :] * jnp.where(below == half, residual[i : i + 1, :], basis)
            lefts[start + i] = left.astype(jnp.bfloat16)
            owns[start + i] = basis.astype(jnp.bfloat16)

    each(0, steps, prepare)

    blank = jnp.zeros((grams.shape[1] - 2 * padded, row_total), jnp.bfloat16)

    def multiply(g):
        swap(g).wait()
        other = tiles_first(other_store, g).astype(jnp.bfloat16)
        start = pl.multiple_of(g * group, group)
        for i in range(group):
            right = jnp.concatenate([owns[start + i], other[i], blank], axis=0)
            row = pl.multiple_of((start + i) * padded, 8)
            grams[pl.ds(row, padded), :] = contract(lefts[start + i], right, ((1,), (1,)))

    each(0, steps, multiply)

    chosen = pulsar_hot.astype(jnp.bfloat16)
    chosen = jnp.concatenate([chosen, chosen], axis=1)
    for j in range(padded):
        into = pl.ds(j, pulsar_total, stride=padded)
        if j > half + 1:
            part_wide[into, :] = jnp.zeros((pulsar_total, part_wide.shape[1]), jnp.float32)
            continue
        if j == half + 1:
            continue
        terms = grams[pl.ds(j, tile_total, stride=padded), :]
        high = terms.astype(jnp.bfloat16)
        low = (terms - high.astype(jnp.float32)).astype(jnp.bfloat16)
        summed = contract(chosen, jnp.concatenate([high, low], axis=0), ((1,), (0,)))
        if j == half:
            coarse = summed.astype(jnp.bfloat16).astype(jnp.float32)
            part_wide[into, :] = coarse
            part_wide[pl.ds(j + 1, pulsar_total, stride=padded), :] = summed - coarse
        else:
            part_wide[into, :] = summed
    part[...] = part_wide[...].reshape(part.shape).astype(jnp.bfloat16)
    each(1, peers, lambda d: part_to(d).start())
    own_rows.wait()
    own_places.wait()

    def take_rows(d):
        rows_to(d).wait()
        places_to(d).wait()

    each(1, peers, take_rows)

    def take(d, acc):
        part_to(d).wait()
        return acc + got_part[d].astype(jnp.float32)

    mine = part[pl.ds(me * owned, owned)].astype(jnp.float32)
    sum_ref[...] = lax.fori_loop(1, peers, take, mine)


def finish_kernel(
    peers,
    half,
    places_ref,
    sum_ref,
    rows_ref,
    gram_ref,
    projection_ref,
    white_ref,
    staged,
):
    first_core = lax.axis_index("rep") == 0
    me = lax.axis_index("toa")
    padded = sum_ref.shape[1]
    per_peer, row_total = rows_ref.shape[1:]
    chunks = row_total // LANES

    def settle(d, carry):
        for i in range(per_peer):
            place = places_ref[d, 0, me * per_peer + i]
            for c in range(chunks):
                staged[c, pl.ds(place, 1), :] = rows_ref[d, i : i + 1, c * LANES : (c + 1) * LANES]
        return carry

    lax.fori_loop(0, peers, settle, 0)
    for c in range(chunks):
        white_ref[:, c * LANES : (c + 1) * LANES] = staged[c]
    for q in range(sum_ref.shape[0]):
        block = sum_ref[q]
        projection_ref[q : q + 1, :] = (
            block[half : half + 1, :half] + block[half + 1 : half + 2, :half]
        )
        mine = block[:half, :half]
        theirs = block[:half, padded : padded + half]
        gram_ref[:, q, :half] = jnp.where(first_core, mine, theirs)
        gram_ref[:, q, half:] = jnp.where(first_core, theirs, mine)


def shards(
    residual, toa_error, basis_rows, efac_table, equad_table, pulsar, backend, counts, owner_slot
):
    tile_total, row_total = residual.shape
    peers = lax.axis_size("toa")
    half = basis_rows.shape[1]
    pulsar_total = efac_table.shape[0]
    owned = pulsar_total // peers
    per_peer = tile_total // peers
    padded = round_up(half + 2, 8)
    width = round_up(2 * padded, LANES)
    steps = tile_total // min(GROUP, tile_total)
    f32 = jnp.float32
    bf16 = jnp.bfloat16
    smem = pl.BlockSpec(memory_space=pltpu.SMEM)
    vmem = pl.BlockSpec(memory_space=pltpu.VMEM)

    def row(vector):
        return vector.reshape(1, tile_total)

    summed, rows, places = pl.pallas_call(
        functools.partial(whole_kernel, peers),
        in_specs=[vmem] * 8 + [pl.BlockSpec(memory_space=pl.ANY)],
        out_specs=[vmem] * 3,
        out_shape=[
            jax.ShapeDtypeStruct((owned, padded, width), f32),
            jax.ShapeDtypeStruct((peers, per_peer, row_total), f32),
            jax.ShapeDtypeStruct((peers, 1, tile_total), jnp.int32),
        ],
        scratch_shapes=[
            pltpu.VMEM((peers, per_peer, row_total), f32),
            pltpu.VMEM((1, tile_total), jnp.int32),
            pltpu.VMEM((half, tile_total, row_total), bf16),
            pltpu.VMEM((half, tile_total, row_total), bf16),
            pltpu.VMEM((tile_total, row_total), f32),
            pltpu.VMEM((tile_total, padded, row_total), bf16),
            pltpu.VMEM((tile_total, padded, row_total), bf16),
            pltpu.VMEM((tile_total * padded, width), f32),
            pltpu.VMEM((pulsar_total * padded, width), f32),
            pltpu.VMEM((pulsar_total, padded, width), bf16),
            pltpu.VMEM((peers, owned, padded, width), bf16),
            pltpu.SemaphoreType.DMA((steps,)),
            pltpu.SemaphoreType.DMA((steps,)),
            pltpu.SemaphoreType.DMA((steps,)),
            pltpu.SemaphoreType.DMA((3, peers)),
            pltpu.SemaphoreType.DMA((3, peers)),
            pltpu.SemaphoreType.DMA((2,)),
        ],
        compiler_params=pltpu.CompilerParams(
            collective_id=0, has_side_effects=True, vmem_limit_bytes=VMEM_ALL
        ),
        name="whole",
    )(
        row(pulsar),
        row(backend),
        row(counts),
        row(owner_slot),
        efac_table,
        equad_table,
        residual,
        toa_error,
        jnp.transpose(basis_rows, (1, 0, 2)),
    )
    gram, projection, whitened = pl.pallas_call(
        functools.partial(finish_kernel, peers, half),
        in_specs=[smem, vmem, vmem],
        out_specs=[vmem] * 3,
        out_shape=[
            jax.ShapeDtypeStruct((half, owned, 2 * half), f32),
            jax.ShapeDtypeStruct((owned, half), f32),
            jax.ShapeDtypeStruct((tile_total, row_total), f32),
        ],
        scratch_shapes=[pltpu.VMEM((row_total // LANES, tile_total, LANES), f32)],
        name="finish",
    )(places, summed, rows)
    return (jnp.transpose(gram, (1, 2, 0)), projection, whitened)


def solution(mesh):
    in_specs = (
        P("toa", None),
        P("toa", None),
        P("toa", "rep", None),
        P(),
        P(),
        P("toa"),
        P("toa"),
        P("toa"),
        P("toa"),
    )
    out_specs = (P("toa", None, "rep"), P("toa", "rep"), P("toa", None))
    return jax.shard_map(shards, mesh=mesh, in_specs=in_specs, out_specs=out_specs, check_vma=False)
```

```python
import functools

import jax
import jax.numpy as jnp
from jax import lax
from jax.experimental import pallas as pl
from jax.experimental.pallas import tpu as pltpu
from jax.sharding import PartitionSpec as P

MESH = pl.DeviceIdType.MESH
GROUP = 16
LANES = 128
VMEM_ALL = 67043328
HIGH = lax.Precision.HIGHEST


def round_up(value, step):
    return (value + step - 1) // step * step


def contract(left, right, dims, precision=None):
    return lax.dot_general(
        left, right, (dims, ((), ())), precision=precision, preferred_element_type=jnp.float32
    )


def whole_kernel(
    peers,
    pulsar_ref,
    backend_ref,
    counts_ref,
    slot_ref,
    efac_ref,
    equad_ref,
    residual_ref,
    error_ref,
    basis_ref,
    sum_ref,
    partner_sum,
    got_rows,
    got_places,
    sorted_rows,
    sorted_places,
    own_store,
    other_store,
    weights,
    lefts,
    owns,
    grams,
    part_wide,
    part,
    got_part,
    load_sems,
    swap_sends,
    swap_arrivals,
    sends,
    arrivals,
    local_sem,
    last_sems,
):
    me = lax.axis_index("toa")
    core = lax.axis_index("rep")
    partner = 1 - core
    half, tile_total, row_total = basis_ref.shape
    padded = lefts.shape[1]
    pulsar_total = efac_ref.shape[0]
    owned = pulsar_total // peers
    per_peer = tile_total // peers
    group = min(GROUP, tile_total)
    steps = tile_total // group
    swaps = steps // 2

    barrier = pltpu.get_barrier_semaphore()
    pl.semaphore_signal(barrier, inc=1, device_id={"rep": partner}, device_id_type=MESH)

    def greet(d, carry):
        pl.semaphore_signal(
            barrier, inc=1, device_id={"toa": lax.rem(me + d, peers)}, device_id_type=MESH
        )
        return carry

    lax.fori_loop(1, peers, greet, 0)

    def chunk(ref, g):
        return ref.at[:, pl.ds(pl.multiple_of(g * group, group), group), :]

    def load(g):
        return pltpu.make_async_copy(chunk(basis_ref, g), chunk(own_store, g), load_sems.at[g])

    def swap(g):
        return pltpu.make_async_remote_copy(
            src_ref=chunk(basis_ref, partner * swaps + g),
            dst_ref=chunk(other_store, g),
            send_sem=swap_sends.at[g],
            recv_sem=swap_arrivals.at[g],
            device_id={"rep": partner},
            device_id_type=MESH,
        )

    def each(first, last, action):
        def body(i, carry):
            action(i)
            return carry

        lax.fori_loop(first, last, body, 0)

    each(0, steps, lambda g: load(g).start())

    def onehot(row, amount):
        index = lax.broadcasted_iota(jnp.int32, (amount, tile_total), 0)
        return (index == row).astype(jnp.float32)

    pulsar_hot = onehot(pulsar_ref[...], pulsar_total)
    backend_hot = onehot(backend_ref[...], efac_ref.shape[1])

    def lookup(ref):
        columns = contract(ref[...], pulsar_hot, ((0,), (0,)), HIGH)
        return jnp.sum(columns * backend_hot, axis=0, keepdims=True)

    factor = lookup(efac_ref)
    floor_term = lookup(equad_ref)
    slot = slot_ref[...]
    dest = slot // tile_total
    place = (slot - dest * tile_total).astype(jnp.float32)
    dest_hot = onehot(dest, peers)
    earlier = (
        lax.broadcasted_iota(jnp.int32, (tile_total, tile_total), 0)
        < lax.broadcasted_iota(jnp.int32, (tile_total, tile_total), 1)
    ).astype(jnp.float32)
    before = contract(dest_hot, earlier, ((1,), (0,)))
    rank = jnp.sum(before * dest_hot, axis=0, keepdims=True)
    position = dest * per_peer + rank.astype(jnp.int32)
    order = onehot(position, tile_total)
    stacked = jnp.concatenate(
        [
            factor * factor,
            floor_term * floor_term,
            counts_ref[...].astype(jnp.float32),
            jnp.zeros((tile_total - 3, tile_total), jnp.float32),
        ],
        axis=0,
    )
    columns = jnp.transpose(stacked)
    lane = lax.broadcasted_iota(jnp.int32, (tile_total, row_total), 1).astype(jnp.float32)
    error = error_ref[...]
    weight = jnp.where(
        lane < columns[:, 2:3], 1.0 / (columns[:, 0:1] * (error * error) + columns[:, 1:2]), 0.0
    )
    weights[...] = weight
    white = jnp.sqrt(weight) * residual_ref[...]
    sorted_rows[...] = contract(order, white, ((1,), (0,)), HIGH).reshape(sorted_rows.shape)
    sorted_places[...] = contract(place, order, ((1,), (1,)), HIGH).astype(jnp.int32)
    own_rows = pltpu.make_async_copy(sorted_rows.at[me], got_rows.at[0], local_sem.at[0])
    own_places = pltpu.make_async_copy(sorted_places, got_places.at[0], local_sem.at[1])
    own_rows.start()
    own_places.start()
    pl.semaphore_wait(barrier, peers)

    def remote(source, target, n, d):
        return pltpu.make_async_remote_copy(
            src_ref=source,
            dst_ref=target,
            send_sem=sends.at[n, d],
            recv_sem=arrivals.at[n, d],
            device_id={"toa": lax.rem(me + d, peers)},
            device_id_type=MESH,
        )

    def rows_to(d):
        return remote(sorted_rows.at[lax.rem(me + d, peers)], got_rows.at[d], 0, d)

    def places_to(d):
        return remote(sorted_places, got_places.at[d], 1, d)

    def part_to(d):
        first = lax.rem(me + d, peers) * owned
        return remote(part.at[pl.ds(first, owned)], got_part.at[d], 2, d)

    each(0, swaps, lambda g: swap(g).start())

    def send_rows(d):
        rows_to(d).start()
        places_to(d).start()

    each(1, peers, send_rows)

    def tiles_first(ref, g):
        block = chunk(ref, g)[...].astype(jnp.float32)
        block = jnp.concatenate(
            [block, jnp.zeros((padded - half, group, row_total), jnp.float32)], axis=0
        )
        return jnp.swapaxes(block, 0, 1)

    below = lax.broadcasted_iota(jnp.int32, (padded, row_total), 0)

    def prepare(g):
        load(g).wait()
        own = tiles_first(own_store, g)
        start = pl.multiple_of(g * group, group)
        weight = weights[pl.ds(start, group), :]
        residual = residual_ref[pl.ds(start, group), :]
        for i in range(group):
            basis = own[i]
            left = weight[i : i + 1, :] * jnp.where(below == half, residual[i : i + 1, :], basis)
            lefts[start + i] = left.astype(jnp.bfloat16)
            owns[start + i] = basis.astype(jnp.bfloat16)

    each(0, steps, prepare)

    blank = jnp.zeros((grams.shape[1] - 2 * padded, row_total), jnp.bfloat16)
    absent = jnp.zeros((grams.shape[1] - padded, row_total), jnp.bfloat16)

    def multiply(tile, rest):
        right = jnp.concatenate([owns[tile]] + rest, axis=0)
        row = pl.multiple_of(tile * padded, 8)
        grams[pl.ds(row, padded), :] = contract(lefts[tile], right, ((1,), (1,)))

    def alone(g):
        for i in range(group):
            multiply((partner * swaps + g) * group + i, [absent])

    def crossed(g):
        swap(g).wait()
        other = tiles_first(other_store, g).astype(jnp.bfloat16)
        for i in range(group):
            multiply((core * swaps + g) * group + i, [other[i], blank])

    each(0, swaps, alone)
    each(0, swaps, crossed)

    chosen = pulsar_hot.astype(jnp.bfloat16)
    chosen = jnp.concatenate([chosen, chosen], axis=1)
    for j in range(padded):
        into = pl.ds(j, pulsar_total, stride=padded)
        if j > half + 1:
            part_wide[into, :] = jnp.zeros((pulsar_total, part_wide.shape[1]), jnp.float32)
            continue
        if j == half + 1:
            continue
        terms = grams[pl.ds(j, tile_total, stride=padded), :]
        high = terms.astype(jnp.bfloat16)
        low = (terms - high.astype(jnp.float32)).astype(jnp.bfloat16)
        summed = contract(chosen, jnp.concatenate([high, low], axis=0), ((1,), (0,)))
        if j == half:
            coarse = summed.astype(jnp.bfloat16).astype(jnp.float32)
            part_wide[into, :] = coarse
            part_wide[pl.ds(j + 1, pulsar_total, stride=padded), :] = summed - coarse
        else:
            part_wide[into, :] = summed
    part[...] = part_wide[...].reshape(part.shape).astype(jnp.bfloat16)
    each(1, peers, lambda d: part_to(d).start())
    own_rows.wait()
    own_places.wait()

    def take_rows(d):
        rows_to(d).wait()
        places_to(d).wait()

    each(1, peers, take_rows)

    def take(d, acc):
        part_to(d).wait()
        return acc + got_part[d].astype(jnp.float32)

    mine = part[pl.ds(me * owned, owned)].astype(jnp.float32)
    sum_ref[...] = lax.fori_loop(1, peers, take, mine)
    last = pltpu.make_async_remote_copy(
        src_ref=sum_ref,
        dst_ref=partner_sum,
        send_sem=last_sems.at[0],
        recv_sem=last_sems.at[1],
        device_id={"rep": partner},
        device_id_type=MESH,
    )
    last.start()
    last.wait()


def finish_kernel(
    peers,
    half,
    places_ref,
    sum_ref,
    partner_ref,
    rows_ref,
    gram_ref,
    projection_ref,
    white_ref,
    staged,
):
    first_core = lax.axis_index("rep") == 0
    me = lax.axis_index("toa")
    padded = sum_ref.shape[1]
    per_peer, row_total = rows_ref.shape[1:]
    chunks = row_total // LANES

    def settle(d, carry):
        for i in range(per_peer):
            place = places_ref[d, 0, me * per_peer + i]
            for c in range(chunks):
                staged[c, pl.ds(place, 1), :] = rows_ref[d, i : i + 1, c * LANES : (c + 1) * LANES]
        return carry

    lax.fori_loop(0, peers, settle, 0)
    for c in range(chunks):
        white_ref[:, c * LANES : (c + 1) * LANES] = staged[c]
    for q in range(sum_ref.shape[0]):
        block = sum_ref[q]
        projection_ref[q : q + 1, :] = (
            block[half : half + 1, :half] + block[half + 1 : half + 2, :half]
        )
        mine = block[:half, :half]
        turned = jnp.transpose(partner_ref[q][:, padded : 2 * padded])
        theirs = block[:half, padded : padded + half] + turned[:half, :half]
        gram_ref[:, q, :half] = jnp.where(first_core, mine, theirs)
        gram_ref[:, q, half:] = jnp.where(first_core, theirs, mine)


def shards(
    residual, toa_error, basis_rows, efac_table, equad_table, pulsar, backend, counts, owner_slot
):
    tile_total, row_total = residual.shape
    peers = lax.axis_size("toa")
    half = basis_rows.shape[1]
    pulsar_total = efac_table.shape[0]
    owned = pulsar_total // peers
    per_peer = tile_total // peers
    padded = round_up(half + 2, 8)
    width = round_up(2 * padded, LANES)
    steps = tile_total // min(GROUP, tile_total)
    f32 = jnp.float32
    bf16 = jnp.bfloat16
    smem = pl.BlockSpec(memory_space=pltpu.SMEM)
    vmem = pl.BlockSpec(memory_space=pltpu.VMEM)

    def row(vector):
        return vector.reshape(1, tile_total)

    summed, partner_summed, rows, places = pl.pallas_call(
        functools.partial(whole_kernel, peers),
        in_specs=[vmem] * 8 + [pl.BlockSpec(memory_space=pl.ANY)],
        out_specs=[vmem] * 4,
        out_shape=[
            jax.ShapeDtypeStruct((owned, padded, width), f32),
            jax.ShapeDtypeStruct((owned, padded, width), f32),
            jax.ShapeDtypeStruct((peers, per_peer, row_total), f32),
            jax.ShapeDtypeStruct((peers, 1, tile_total), jnp.int32),
        ],
        scratch_shapes=[
            pltpu.VMEM((peers, per_peer, row_total), f32),
            pltpu.VMEM((1, tile_total), jnp.int32),
            pltpu.VMEM((half, tile_total, row_total), bf16),
            pltpu.VMEM((half, tile_total // 2, row_total), bf16),
            pltpu.VMEM((tile_total, row_total), f32),
            pltpu.VMEM((tile_total, padded, row_total), bf16),
            pltpu.VMEM((tile_total, padded, row_total), bf16),
            pltpu.VMEM((tile_total * padded, width), f32),
            pltpu.VMEM((pulsar_total * padded, width), f32),
            pltpu.VMEM((pulsar_total, padded, width), bf16),
            pltpu.VMEM((peers, owned, padded, width), bf16),
            pltpu.SemaphoreType.DMA((steps,)),
            pltpu.SemaphoreType.DMA((steps // 2,)),
            pltpu.SemaphoreType.DMA((steps // 2,)),
            pltpu.SemaphoreType.DMA((3, peers)),
            pltpu.SemaphoreType.DMA((3, peers)),
            pltpu.SemaphoreType.DMA((2,)),
            pltpu.SemaphoreType.DMA((2,)),
        ],
        compiler_params=pltpu.CompilerParams(
            collective_id=0, has_side_effects=True, vmem_limit_bytes=VMEM_ALL
        ),
        name="whole",
    )(
        row(pulsar),
        row(backend),
        row(counts),
        row(owner_slot),
        efac_table,
        equad_table,
        residual,
        toa_error,
        jnp.transpose(basis_rows, (1, 0, 2)),
    )
    gram, projection, whitened = pl.pallas_call(
        functools.partial(finish_kernel, peers, half),
        in_specs=[smem, vmem, vmem, vmem],
        out_specs=[vmem] * 3,
        out_shape=[
            jax.ShapeDtypeStruct((half, owned, 2 * half), f32),
            jax.ShapeDtypeStruct((owned, half), f32),
            jax.ShapeDtypeStruct((tile_total, row_total), f32),
        ],
        scratch_shapes=[pltpu.VMEM((row_total // LANES, tile_total, LANES), f32)],
        name="finish",
    )(places, summed, partner_summed, rows)
    return (jnp.transpose(gram, (1, 2, 0)), projection, whitened)


def solution(mesh):
    in_specs = (
        P("toa", None),
        P("toa", None),
        P("toa", "rep", None),
        P(),
        P(),
        P("toa"),
        P("toa"),
        P("toa"),
        P("toa"),
    )
    out_specs = (P("toa", None, "rep"), P("toa", "rep"), P("toa", None))
    return jax.shard_map(shards, mesh=mesh, in_specs=in_specs, out_specs=out_specs, check_vma=False)
```

```python
import functools

import jax
import jax.numpy as jnp
from jax import lax
from jax.experimental import pallas as pl
from jax.experimental.pallas import tpu as pltpu
from jax.sharding import PartitionSpec as P

MESH = pl.DeviceIdType.MESH
GROUP = 16
LANES = 128
VMEM_ALL = 67043328
HIGH = lax.Precision.HIGHEST


def round_up(value, step):
    return (value + step - 1) // step * step


def contract(left, right, dims, precision=None):
    return lax.dot_general(
        left, right, (dims, ((), ())), precision=precision, preferred_element_type=jnp.float32
    )


def whole_kernel(
    peers,
    pulsar_ref,
    backend_ref,
    counts_ref,
    slot_ref,
    efac_ref,
    equad_ref,
    residual_ref,
    error_ref,
    basis_ref,
    sum_ref,
    partner_sum,
    got_rows,
    got_places,
    sorted_rows,
    sorted_places,
    own_store,
    other_store,
    weights,
    lefts,
    owns,
    grams,
    part_wide,
    part,
    got_part,
    load_sems,
    swap_sends,
    swap_arrivals,
    sends,
    arrivals,
    local_sem,
    last_sems,
):
    me = lax.axis_index("toa")
    core = lax.axis_index("rep")
    partner = 1 - core
    half, tile_total, row_total = basis_ref.shape
    padded = lefts.shape[1]
    pulsar_total = efac_ref.shape[0]
    owned = pulsar_total // peers
    per_peer = tile_total // peers
    group = min(GROUP, tile_total)
    steps = tile_total // group
    swaps = steps // 2

    barrier = pltpu.get_barrier_semaphore()
    pl.semaphore_signal(barrier, inc=1, device_id={"rep": partner}, device_id_type=MESH)

    def greet(d, carry):
        pl.semaphore_signal(
            barrier, inc=1, device_id={"toa": lax.rem(me + d, peers)}, device_id_type=MESH
        )
        return carry

    lax.fori_loop(1, peers, greet, 0)

    def chunk(ref, g):
        return ref.at[:, pl.ds(pl.multiple_of(g * group, group), group), :]

    def load(g):
        return pltpu.make_async_copy(chunk(basis_ref, g), chunk(own_store, g), load_sems.at[g])

    def swap(g):
        return pltpu.make_async_remote_copy(
            src_ref=chunk(basis_ref, partner * swaps + g),
            dst_ref=chunk(other_store, g),
            send_sem=swap_sends.at[g],
            recv_sem=swap_arrivals.at[g],
            device_id={"rep": partner},
            device_id_type=MESH,
        )

    def each(first, last, action):
        def body(i, carry):
            action(i)
            return carry

        lax.fori_loop(first, last, body, 0)

    each(0, steps, lambda g: load(g).start())

    def onehot(row, amount):
        index = lax.broadcasted_iota(jnp.int32, (amount, tile_total), 0)
        return (index == row).astype(jnp.float32)

    pulsar_hot = onehot(pulsar_ref[...], pulsar_total)
    backend_hot = onehot(backend_ref[...], efac_ref.shape[1])

    def lookup(ref):
        columns = contract(ref[...], pulsar_hot, ((0,), (0,)), HIGH)
        return jnp.sum(columns * backend_hot, axis=0, keepdims=True)

    factor = lookup(efac_ref)
    floor_term = lookup(equad_ref)
    slot = slot_ref[...]
    dest = slot // tile_total
    place = (slot - dest * tile_total).astype(jnp.float32)
    dest_hot = onehot(dest, peers)
    earlier = (
        lax.broadcasted_iota(jnp.int32, (tile_total, tile_total), 0)
        < lax.broadcasted_iota(jnp.int32, (tile_total, tile_total), 1)
    ).astype(jnp.float32)
    before = contract(dest_hot, earlier, ((1,), (0,)))
    rank = jnp.sum(before * dest_hot, axis=0, keepdims=True)
    position = dest * per_peer + rank.astype(jnp.int32)
    order = onehot(position, tile_total)
    stacked = jnp.concatenate(
        [
            factor * factor,
            floor_term * floor_term,
            counts_ref[...].astype(jnp.float32),
            jnp.zeros((tile_total - 3, tile_total), jnp.float32),
        ],
        axis=0,
    )
    columns = jnp.transpose(stacked)
    lane = lax.broadcasted_iota(jnp.int32, (tile_total, row_total), 1).astype(jnp.float32)
    error = error_ref[...]
    weight = jnp.where(
        lane < columns[:, 2:3], 1.0 / (columns[:, 0:1] * (error * error) + columns[:, 1:2]), 0.0
    )
    weights[...] = weight
    white = jnp.sqrt(weight) * residual_ref[...]
    sorted_rows[...] = contract(order, white, ((1,), (0,)), HIGH).reshape(sorted_rows.shape)
    sorted_places[...] = contract(place, order, ((1,), (1,)), HIGH).astype(jnp.int32)
    own_rows = pltpu.make_async_copy(sorted_rows.at[me], got_rows.at[0], local_sem.at[0])
    own_places = pltpu.make_async_copy(sorted_places, got_places.at[0], local_sem.at[1])
    own_rows.start()
    own_places.start()

    def tiles_first(ref, g):
        block = chunk(ref, g)[...].astype(jnp.float32)
        block = jnp.concatenate(
            [block, jnp.zeros((padded - half, group, row_total), jnp.float32)], axis=0
        )
        return jnp.swapaxes(block, 0, 1)

    below = lax.broadcasted_iota(jnp.int32, (padded, row_total), 0)

    def prepare(g):
        load(g).wait()
        own = tiles_first(own_store, g)
        start = pl.multiple_of(g * group, group)
        weight = weights[pl.ds(start, group), :]
        residual = residual_ref[pl.ds(start, group), :]
        for i in range(group):
            basis = own[i]
            left = weight[i : i + 1, :] * jnp.where(below == half, residual[i : i + 1, :], basis)
            lefts[start + i] = left.astype(jnp.bfloat16)
            owns[start + i] = basis.astype(jnp.bfloat16)

    each(0, steps, prepare)
    pl.semaphore_wait(barrier, peers)

    def remote(source, target, n, d):
        return pltpu.make_async_remote_copy(
            src_ref=source,
            dst_ref=target,
            send_sem=sends.at[n, d],
            recv_sem=arrivals.at[n, d],
            device_id={"toa": lax.rem(me + d, peers)},
            device_id_type=MESH,
        )

    def rows_to(d):
        return remote(sorted_rows.at[lax.rem(me + d, peers)], got_rows.at[d], 0, d)

    def places_to(d):
        return remote(sorted_places, got_places.at[d], 1, d)

    def part_to(d):
        first = lax.rem(me + d, peers) * owned
        return remote(part.at[pl.ds(first, owned)], got_part.at[d], 2, d)

    each(0, swaps, lambda g: swap(g).start())

    def send_rows(d):
        rows_to(d).start()
        places_to(d).start()

    each(1, peers, send_rows)

    blank = jnp.zeros((grams.shape[1] - 2 * padded, row_total), jnp.bfloat16)
    absent = jnp.zeros((grams.shape[1] - padded, row_total), jnp.bfloat16)

    def multiply(tile, rest):
        right = jnp.concatenate([owns[tile]] + rest, axis=0)
        row = pl.multiple_of(tile * padded, 8)
        grams[pl.ds(row, padded), :] = contract(lefts[tile], right, ((1,), (1,)))

    def alone(g):
        for i in range(group):
            multiply((partner * swaps + g) * group + i, [absent])

    def crossed(g):
        swap(g).wait()
        other = tiles_first(other_store, g).astype(jnp.bfloat16)
        for i in range(group):
            multiply((core * swaps + g) * group + i, [other[i], blank])

    each(0, swaps, alone)
    each(0, swaps, crossed)

    chosen = pulsar_hot.astype(jnp.bfloat16)
    chosen = jnp.concatenate([chosen, chosen], axis=1)
    for j in range(padded):
        into = pl.ds(j, pulsar_total, stride=padded)
        if j > half + 1:
            part_wide[into, :] = jnp.zeros((pulsar_total, part_wide.shape[1]), jnp.float32)
            continue
        if j == half + 1:
            continue
        terms = grams[pl.ds(j, tile_total, stride=padded), :]
        high = terms.astype(jnp.bfloat16)
        low = (terms - high.astype(jnp.float32)).astype(jnp.bfloat16)
        summed = contract(chosen, jnp.concatenate([high, low], axis=0), ((1,), (0,)))
        if j == half:
            coarse = summed.astype(jnp.bfloat16).astype(jnp.float32)
            part_wide[into, :] = coarse
            part_wide[pl.ds(j + 1, pulsar_total, stride=padded), :] = summed - coarse
        else:
            part_wide[into, :] = summed
    part[...] = part_wide[...].reshape(part.shape).astype(jnp.bfloat16)
    each(1, peers, lambda d: part_to(d).start())
    own_rows.wait()
    own_places.wait()

    def take_rows(d):
        rows_to(d).wait()
        places_to(d).wait()

    each(1, peers, take_rows)

    def take(d, acc):
        part_to(d).wait()
        return acc + got_part[d].astype(jnp.float32)

    mine = part[pl.ds(me * owned, owned)].astype(jnp.float32)
    sum_ref[...] = lax.fori_loop(1, peers, take, mine)
    last = pltpu.make_async_remote_copy(
        src_ref=sum_ref,
        dst_ref=partner_sum,
        send_sem=last_sems.at[0],
        recv_sem=last_sems.at[1],
        device_id={"rep": partner},
        device_id_type=MESH,
    )
    last.start()
    last.wait()


def finish_kernel(
    peers,
    half,
    places_ref,
    sum_ref,
    partner_ref,
    rows_ref,
    gram_ref,
    projection_ref,
    white_ref,
    staged,
):
    first_core = lax.axis_index("rep") == 0
    me = lax.axis_index("toa")
    padded = sum_ref.shape[1]
    per_peer, row_total = rows_ref.shape[1:]
    chunks = row_total // LANES

    def settle(d, carry):
        for i in range(per_peer):
            place = places_ref[d, 0, me * per_peer + i]
            for c in range(chunks):
                staged[c, pl.ds(place, 1), :] = rows_ref[d, i : i + 1, c * LANES : (c + 1) * LANES]
        return carry

    lax.fori_loop(0, peers, settle, 0)
    for c in range(chunks):
        white_ref[:, c * LANES : (c + 1) * LANES] = staged[c]
    for q in range(sum_ref.shape[0]):
        block = sum_ref[q]
        projection_ref[q : q + 1, :] = (
            block[half : half + 1, :half] + block[half + 1 : half + 2, :half]
        )
        mine = block[:half, :half]
        turned = jnp.transpose(partner_ref[q][:, padded : 2 * padded])
        theirs = block[:half, padded : padded + half] + turned[:half, :half]
        gram_ref[:, q, :half] = jnp.where(first_core, mine, theirs)
        gram_ref[:, q, half:] = jnp.where(first_core, theirs, mine)


def shards(
    residual, toa_error, basis_rows, efac_table, equad_table, pulsar, backend, counts, owner_slot
):
    tile_total, row_total = residual.shape
    peers = lax.axis_size("toa")
    half = basis_rows.shape[1]
    pulsar_total = efac_table.shape[0]
    owned = pulsar_total // peers
    per_peer = tile_total // peers
    padded = round_up(half + 2, 8)
    width = round_up(2 * padded, LANES)
    steps = tile_total // min(GROUP, tile_total)
    f32 = jnp.float32
    bf16 = jnp.bfloat16
    smem = pl.BlockSpec(memory_space=pltpu.SMEM)
    vmem = pl.BlockSpec(memory_space=pltpu.VMEM)

    def row(vector):
        return vector.reshape(1, tile_total)

    summed, partner_summed, rows, places = pl.pallas_call(
        functools.partial(whole_kernel, peers),
        in_specs=[vmem] * 8 + [pl.BlockSpec(memory_space=pl.ANY)],
        out_specs=[vmem] * 4,
        out_shape=[
            jax.ShapeDtypeStruct((owned, padded, width), f32),
            jax.ShapeDtypeStruct((owned, padded, width), f32),
            jax.ShapeDtypeStruct((peers, per_peer, row_total), f32),
            jax.ShapeDtypeStruct((peers, 1, tile_total), jnp.int32),
        ],
        scratch_shapes=[
            pltpu.VMEM((peers, per_peer, row_total), f32),
            pltpu.VMEM((1, tile_total), jnp.int32),
            pltpu.VMEM((half, tile_total, row_total), bf16),
            pltpu.VMEM((half, tile_total // 2, row_total), bf16),
            pltpu.VMEM((tile_total, row_total), f32),
            pltpu.VMEM((tile_total, padded, row_total), bf16),
            pltpu.VMEM((tile_total, padded, row_total), bf16),
            pltpu.VMEM((tile_total * padded, width), f32),
            pltpu.VMEM((pulsar_total * padded, width), f32),
            pltpu.VMEM((pulsar_total, padded, width), bf16),
            pltpu.VMEM((peers, owned, padded, width), bf16),
            pltpu.SemaphoreType.DMA((steps,)),
            pltpu.SemaphoreType.DMA((steps // 2,)),
            pltpu.SemaphoreType.DMA((steps // 2,)),
            pltpu.SemaphoreType.DMA((3, peers)),
            pltpu.SemaphoreType.DMA((3, peers)),
            pltpu.SemaphoreType.DMA((2,)),
            pltpu.SemaphoreType.DMA((2,)),
        ],
        compiler_params=pltpu.CompilerParams(
            collective_id=0, has_side_effects=True, vmem_limit_bytes=VMEM_ALL
        ),
        name="whole",
    )(
        row(pulsar),
        row(backend),
        row(counts),
        row(owner_slot),
        efac_table,
        equad_table,
        residual,
        toa_error,
        jnp.transpose(basis_rows, (1, 0, 2)),
    )
    gram, projection, whitened = pl.pallas_call(
        functools.partial(finish_kernel, peers, half),
        in_specs=[smem, vmem, vmem, vmem],
        out_specs=[vmem] * 3,
        out_shape=[
            jax.ShapeDtypeStruct((half, owned, 2 * half), f32),
            jax.ShapeDtypeStruct((owned, half), f32),
            jax.ShapeDtypeStruct((tile_total, row_total), f32),
        ],
        scratch_shapes=[pltpu.VMEM((row_total // LANES, tile_total, LANES), f32)],
        name="finish",
    )(places, summed, partner_summed, rows)
    return (jnp.transpose(gram, (1, 2, 0)), projection, whitened)


def solution(mesh):
    in_specs = (
        P("toa", None),
        P("toa", None),
        P("toa", "rep", None),
        P(),
        P(),
        P("toa"),
        P("toa"),
        P("toa"),
        P("toa"),
    )
    out_specs = (P("toa", None, "rep"), P("toa", "rep"), P("toa", None))
    return jax.shard_map(shards, mesh=mesh, in_specs=in_specs, out_specs=out_specs, check_vma=False)
```
